32 devices in a mesh: seq: 8 (over y, x, core), head: 4 (over z).
Axes of the slice: x: 2, y: 2, z: 4, core: 2. Of those that a mesh axis runs over, the one named last changes fastest.
Arguments:
- queries: bfloat16 [4096, 2048], P('seq', 'head'), may hold values from -6 to 6
- key_rows: bfloat16 [4096, 2048], P('seq', 'head'), may hold values from -6 to 6
- values: bfloat16 [4096, 2048], P('seq', 'head'), may hold values from -6 to 6
- write_rate: float32 [16, 4096], P('head', 'seq'), may hold values from 0.001 to 0.95
- decay_rate: float32 [16, 4096], P('head', 'seq'), may hold values from 0 to 1.5
- level_weight: int32 [64, 7], P('seq'), may hold values from 1 to 64
- out_weight: bfloat16 [2048, 2048], P('head'), may hold values from -0.125 to 0.125
Outputs:
- mixed_out: bfloat16 [4096, 2048], P(('seq', 'head'))
The draws below stay inside these ranges and needn't reach their ends.
All inputs are finite; a program needn't handle non-finite values.
Results may differ from the reference program's by a relative error of at most 0.0049.
Values sent between devices are 32-bit elements; how exact they have to be, the bound alone decides.
A program may use at most 128 MiB of HBM per device.

```python
import jax
import jax.numpy as jnp
import numpy as np
from jax import lax

D = 2048
HEAD_COUNT = 16
DK = 128
BLOCK = 64
NCH = 64
STREAM_TOKENS = 4096
LEVELS = 7


def draw_write_rate(key, part):
    key_base, key_token = jax.random.split(key)
    base_rate = jnp.exp(jax.random.uniform(key_base, (HEAD_COUNT, 1), jnp.float32, jnp.log(0.003), jnp.log(0.5)))
    factor = jnp.exp(jax.random.uniform(key_token, (HEAD_COUNT, STREAM_TOKENS), jnp.float32, jnp.log(0.5), jnp.log(2.0)))
    return jnp.minimum(base_rate * factor, 0.95)


def draw_decay_rate(key, part):
    key_base, key_block, key_token, key_location = jax.random.split(key, 4)
    low_rate = jnp.log(0.3 / STREAM_TOKENS)
    high_rate = jnp.log(0.03)
    base_rate = jnp.exp(jax.random.uniform(key_base, (HEAD_COUNT, 1, 1), jnp.float32, low_rate, high_rate))
    block_factor = jnp.exp(jax.random.uniform(key_block, (HEAD_COUNT, NCH, 1), jnp.float32, jnp.log(0.5), jnp.log(2.0)))
    token_factor = jax.random.uniform(key_token, (HEAD_COUNT, NCH, BLOCK), jnp.float32, 0.5, 1.5)
    smoothed_signal = (base_rate * block_factor * token_factor).reshape(HEAD_COUNT, STREAM_TOKENS)
    spike_locations = jax.random.randint(key_location, (HEAD_COUNT, 4, 1), 0, STREAM_TOKENS)
    token_offsets = jnp.arange(STREAM_TOKENS, dtype=jnp.int32).reshape(1, 1, STREAM_TOKENS)
    spike_events = jnp.sum(jnp.where(spike_locations == token_offsets, 0.35, 0.0), axis=1)
    return smoothed_signal + spike_events


def with_ends(result, rng, least, top_value):
    extent = result.shape
    place = [jax.random.randint(jax.random.fold_in(rng, axis), (), 0, extent[axis]) for axis in range(len(extent))]
    result = result.at[tuple(place)].set(least)
    longest = extent.index(max(extent))
    place[longest] = (place[longest] + 1) % extent[longest]
    return result.at[tuple(place)].set(top_value)


def block_levels(key, shape, cuts, least, high):
    def one(position, blocks):
        heights = jax.random.uniform(jax.random.fold_in(jax.random.fold_in(key, 6), position), (blocks,), jnp.float32, least / len(cuts), high / len(cuts))
        return jnp.repeat(jnp.exp(heights), shape[position] // blocks).reshape((-1,) + (1,) * (len(shape) - position - 1))

    level = one(*cuts[0])
    for cut in cuts[1:]:
        level = level * one(*cut)
    return level


def bell_draw(rng, dims, scale, limit, shards=(), kind=jnp.bfloat16):
    drawn = scale * jax.random.normal(rng, dims, jnp.float32)
    if shards:
        drawn = drawn * block_levels(rng, dims, shards, -0.22, 0.18)
    return jnp.clip(drawn, -limit, limit).astype(kind)


def setup_inputs(seed: int = 0) -> dict:
    seeds = jax.random.split(jax.random.key(seed), 8)
    queries = bell_draw(seeds[0], (STREAM_TOKENS, HEAD_COUNT * DK), 1.0, 6.0, ((0, 8), (1, 4)))
    key_rows = bell_draw(seeds[1], (STREAM_TOKENS, HEAD_COUNT * DK), 1.0, 6.0, ((0, 8), (1, 4)))
    values = bell_draw(seeds[2], (STREAM_TOKENS, HEAD_COUNT * DK), 1.0, 6.0, ((0, 8), (1, 4)))
    write_rate = draw_write_rate(jax.random.fold_in(seeds[7], 71), 0)
    decay_rate = draw_decay_rate(jax.random.fold_in(seeds[7], 71), 0)
    level_weight = with_ends(jax.random.randint(seeds[5], (NCH, LEVELS), 1, 65), jax.random.fold_in(seeds[5], 1), 1, 64).astype(jnp.int32)
    out_weight = bell_draw(seeds[6], (HEAD_COUNT * DK, D), (HEAD_COUNT * DK) ** -0.5, 0.125, ((0, 4),))
    return dict(queries=queries, key_rows=key_rows, values=values, write_rate=write_rate, decay_rate=decay_rate, level_weight=level_weight, out_weight=out_weight)


HIGHEST_MODE = lax.Precision.HIGHEST
NORM_EPS = 1e-06
LEVEL_UNIT = 0.125

def unit_rows(matrix):
    return matrix * lax.rsqrt(lax.optimization_barrier(jnp.sum(matrix * matrix, axis=-1, keepdims=True)) + NORM_EPS)

def mat_prod(left, right):
    return jnp.matmul(left, right, precision=HIGHEST_MODE)

def block_terms(queries, key_rows, values, write_rate, decay_rate):
    length = queries.shape[-2]
    log_decay = -jnp.cumsum(decay_rate, axis=-1)
    later_pos = jnp.arange(length)[:, None]
    earlier_pos = jnp.arange(length)[None, :]
    causal = later_pos >= earlier_pos
    strictly = later_pos > earlier_pos
    spread_log = log_decay[..., :, None] - log_decay[..., None, :]
    ratios = jnp.where(causal, jnp.exp(jnp.where(causal, spread_log, 0.0)), 0.0)
    key_gram = mat_prod(key_rows, jnp.swapaxes(key_rows, -1, -2))
    nilpotent = jnp.where(strictly, write_rate[..., :, None] * ratios * key_gram, 0.0)
    eye_block = jnp.eye(length, dtype=jnp.float32)
    inverse = eye_block - nilpotent
    powered = nilpotent
    for doubling in range(1, (length - 1).bit_length()):
        powered = mat_prod(powered, powered)
        inverse = mat_prod(inverse, eye_block + powered)
    gammas = jnp.exp(log_decay)
    to_end = jnp.exp(log_decay[..., -1:] - log_decay)
    w_value = mat_prod(inverse, write_rate[..., None] * values)
    w_key = mat_prod(inverse, (write_rate * gammas)[..., None] * key_rows)
    keys_tail = jnp.swapaxes(key_rows * to_end[..., None], -1, -2)
    eye_state = jnp.eye(key_rows.shape[-1], dtype=jnp.float32)
    carry_map = gammas[..., -1:, None] * eye_state - mat_prod(keys_tail, w_key)
    carry_add = mat_prod(keys_tail, w_value)
    scores = mat_prod(queries, jnp.swapaxes(key_rows, -1, -2)) * ratios
    from_prior = gammas[..., None] * queries - mat_prod(scores, w_key)
    inside = mat_prod(scores, w_value)
    return (carry_map, carry_add, from_prior, inside)

def compose(left_map, left_add, right_map, right_add):
    return (mat_prod(right_map, left_map), mat_prod(right_map, left_add) + right_add)

def build_levels(span_map, span_add):
    levels = [(span_map, span_add)]
    while span_map.shape[0] > 1:
        span_map, span_add = compose(span_map[0::2], span_add[0::2], span_map[1::2], span_add[1::2])
        levels.append((span_map, span_add))
    return levels

def fold_levels(levels, weights, folded):
    stretch_count = folded.shape[0]
    stretch_index = np.arange(stretch_count)
    shape_tail = (stretch_count,) + (1,) * (folded.ndim - 1)
    for depth_bit in reversed(range(len(levels))):
        span_map, span_add = levels[depth_bit]
        bit_set = (stretch_index >> depth_bit & 1).astype(bool).reshape(shape_tail)
        pick_idx = np.maximum((stretch_index >> depth_bit) - 1, 0)
        level_scale = weights[:, 1 + depth_bit].reshape(shape_tail)
        stepped = mat_prod(span_map[pick_idx], folded) + level_scale * span_add[pick_idx]
        folded = jnp.where(bit_set, stepped, folded)
    return folded

def reference(queries, key_rows, values, write_rate, decay_rate, level_weight, out_weight):
    stretch_count = STREAM_TOKENS // BLOCK
    weights = level_weight.astype(jnp.float32) * LEVEL_UNIT

    def arrange(matrix):
        return jnp.transpose(matrix.reshape(stretch_count, BLOCK, HEAD_COUNT, DK), (2, 0, 1, 3))

    def one_head(head_items):
        query_part, key_part, value_part, rate_part, decay_part = head_items
        carry_map, carry_add, from_prior, inside = block_terms(unit_rows(query_part.astype(jnp.float32)), unit_rows(key_part.astype(jnp.float32)), value_part.astype(jnp.float32), rate_part.reshape(stretch_count, BLOCK), decay_part.reshape(stretch_count, BLOCK))
        levels = build_levels(carry_map, carry_add)
        folded = fold_levels(levels[:-1], weights, jnp.zeros((stretch_count, DK, DK), jnp.float32))
        return mat_prod(from_prior, folded) + weights[:, 0].reshape(stretch_count, 1, 1) * inside
    head_rows = lax.map(one_head, (arrange(queries), arrange(key_rows), arrange(values), write_rate, decay_rate))
    heads_out = jnp.transpose(head_rows, (1, 2, 0, 3)).reshape(STREAM_TOKENS, HEAD_COUNT * DK).astype(jnp.bfloat16)
    return jnp.dot(heads_out, out_weight, preferred_element_type=jnp.float32).astype(jnp.bfloat16)
```

```python
import functools

import jax
import jax.numpy as jnp
from jax import lax
from jax.experimental import pallas as pl
from jax.experimental.pallas import tpu as pltpu
from jax.sharding import PartitionSpec as P

BLOCK = 64
NORM_EPS = 1e-06
LEVEL_UNIT = 0.125
F32 = jnp.float32
BF16 = jnp.bfloat16
NN = (((1,), (0,)), ((), ()))
NT = (((1,), (1,)), ((), ()))
TN = (((0,), (0,)), ((), ()))


def dot(left, right, dims=NN):
    return lax.dot_general(left, right, dims, preferred_element_type=F32)


def exact_dot(left, right, dims=NN):
    return lax.dot_general(
        left, right, dims, precision=lax.Precision.HIGHEST, preferred_element_type=F32
    )


def split(x):
    high = x.astype(BF16)
    return high, (x - high.astype(F32)).astype(BF16)


def dot3(left, right):
    (lh, ll), (rh, rl) = left, right
    return dot(lh, rh) + (dot(lh, rl) + dot(ll, rh))


def local_kernel(q_ref, k_ref, v_ref, beta_ref, decay_ref, lw_ref, g_ref, o_ref, ab_ref):
    blocks = q_ref.shape[0] // BLOCK
    size = q_ref.shape[1]
    every = range(blocks)
    row_at = lax.broadcasted_iota(jnp.int32, (BLOCK, BLOCK), 0)
    col_at = lax.broadcasted_iota(jnp.int32, (BLOCK, BLOCK), 1)
    causal, strictly, diag = row_at >= col_at, row_at > col_at, row_at == col_at
    lower = jnp.where(causal, 1.0, 0.0).astype(F32)
    eye = jnp.where(diag, 1.0, 0.0).astype(F32)
    beta_rows = beta_ref[0]
    decay_rows = decay_ref[0]
    log_rows = -exact_dot(decay_rows, lower, NT)
    log_cols = -exact_dot(lower, decay_rows, NT)
    beta_cols = exact_dot(eye, beta_rows, NT)

    q = [q_ref[c * BLOCK : (c + 1) * BLOCK, :] for c in every]
    k = [k_ref[c * BLOCK : (c + 1) * BLOCK, :] for c in every]
    v = [v_ref[c * BLOCK : (c + 1) * BLOCK, :] for c in every]
    power, inverse, scores, pre = [], [], [], []
    for c in every:
        log_row, log_col = log_rows[c : c + 1, :], log_cols[:, c : c + 1]
        gram = dot(k[c], k[c], NT)
        on_diag = jnp.where(diag, gram, 0.0)
        rk_row = lax.rsqrt(jnp.sum(on_diag, axis=0, keepdims=True) + NORM_EPS)
        rk_col = lax.rsqrt(jnp.sum(on_diag, axis=1, keepdims=True) + NORM_EPS)
        qf = q[c].astype(F32)
        rq_col = lax.rsqrt(jnp.sum(qf * qf, axis=1, keepdims=True) + NORM_EPS)
        ratios = jnp.where(causal, jnp.exp(jnp.where(causal, log_col - log_row, 0.0)), 0.0)
        scaled = ratios * rk_row
        n = jnp.where(strictly, (beta_cols[:, c : c + 1] * rk_col) * (scaled * gram), 0.0)
        power.append(n)
        inverse.append(eye - n)
        scores.append(dot(q[c], k[c], NT) * (scaled * rq_col))
        end = log_row[:, BLOCK - 1 :]
        pre.append((
            beta_rows[c : c + 1, :] * rk_row * jnp.exp(log_row),
            beta_rows[c : c + 1, :],
            rk_col * jnp.exp(end - log_col),
            jnp.exp(log_col) * rq_col * qf,
            jnp.exp(end),
        ))
    steps = (BLOCK - 1).bit_length() - 1
    for c in every:
        ph, plo = split(power[c])
        power[c] = dot3((ph, plo), (ph, plo))
    for step in range(steps):
        for c in every:
            ph, plo = split(power[c])
            ih, ilo = split(inverse[c])
            if step < steps - 1:
                out = dot3(
                    (jnp.concatenate([ph, ih], 0), jnp.concatenate([plo, ilo], 0)), (ph, plo)
                )
                power[c] = out[:BLOCK]
                inverse[c] = inverse[c] + out[BLOCK:]
            else:
                inverse[c] = inverse[c] + dot3((ih, ilo), (ph, plo))
    maps, fronts, inside = [], [], []
    eye_state = jnp.where(
        lax.broadcasted_iota(jnp.int32, (size, size), 0)
        == lax.broadcasted_iota(jnp.int32, (size, size), 1),
        1.0,
        0.0,
    ).astype(F32)
    for c in every:
        key_scale, value_scale, tail_scale, q_part, gamma_end = pre[c]
        kh, kl = split(inverse[c] * key_scale)
        vh, vl = split(inverse[c] * value_scale)
        w = jnp.concatenate([dot(kh, k[c]) + dot(kl, k[c]), dot(vh, v[c]) + dot(vl, v[c])], 1)
        th, tl = split(w * tail_scale)
        carry = dot(k[c], th, TN) + dot(k[c], tl, TN)
        maps.append(
            jnp.concatenate([gamma_end * eye_state - carry[:, :size], carry[:, size:]], 1)
        )
        reads = dot3(split(scores[c]), split(w))
        fronts.append(q_part - reads[:, :size])
        inside.append(reads[:, size:])
    levels = [maps]
    while len(maps) > 1:
        merged = []
        for left, right in zip(maps[0::2], maps[1::2]):
            out = dot3(split(right[:, :size]), split(left))
            merged.append(
                jnp.concatenate([out[:, :size], out[:, size:] + right[:, size:]], 1)
            )
        maps = merged
        levels.append(maps)
    ab_ref[0] = levels[-1][0]
    splits = [[split(m) for m in level] for level in levels[:-1]]
    for c in every:
        front = fronts[c]
        total = lw_ref[c, 0].astype(F32) * LEVEL_UNIT * inside[c]
        for bit in range(len(splits)):
            if c >> bit & 1:
                out = dot3(split(front), splits[bit][(c >> bit) - 1])
                total = total + lw_ref[c, 1 + bit].astype(F32) * LEVEL_UNIT * out[:, size:]
                front = out[:, :size]
        g_ref[c * BLOCK : (c + 1) * BLOCK, :] = front
        o_ref[c * BLOCK : (c + 1) * BLOCK, :] = total


def local_part(queries, key_rows, values, write_rate, decay_rate, level_weight):
    heads = write_rate.shape[0]
    tokens = queries.shape[0]
    size = queries.shape[1] // heads
    blocks = tokens // BLOCK
    wide = pl.BlockSpec((tokens, size), lambda h: (0, h))
    rates = pl.BlockSpec((1, blocks, BLOCK), lambda h: (h, 0, 0))
    return pl.pallas_call(
        local_kernel,
        grid=(heads,),
        in_specs=[wide, wide, wide, rates, rates, pl.BlockSpec(memory_space=pltpu.SMEM)],
        out_specs=[wide, wide, pl.BlockSpec((1, size, 2 * size), lambda h: (h, 0, 0))],
        out_shape=[
            jax.ShapeDtypeStruct((tokens, heads * size), F32),
            jax.ShapeDtypeStruct((tokens, heads * size), F32),
            jax.ShapeDtypeStruct((heads, size, 2 * size), F32),
        ],
        name="local_part",
    )(
        queries,
        key_rows,
        values,
        write_rate.reshape(heads, blocks, BLOCK),
        decay_rate.reshape(heads, blocks, BLOCK),
        level_weight,
    )


def per_device(queries, key_rows, values, write_rate, decay_rate, level_weight, out_weight):
    heads = write_rate.shape[0]
    tokens = queries.shape[0]
    size = queries.shape[1] // heads
    blocks = tokens // BLOCK
    depth = blocks.bit_length() - 1
    front, total, pair = local_part(
        queries, key_rows, values, write_rate, decay_rate, level_weight
    )
    mm = functools.partial(jnp.matmul, precision=lax.Precision.HIGHEST)
    spans = lax.all_gather(pair[None], "seq", axis=0, tiled=True)
    place = lax.axis_index("seq")
    bits = lax.axis_size("seq").bit_length() - 1
    levels = [spans]
    for _ in range(bits - 1):
        left, right = spans[0::2], spans[1::2]
        out = mm(right[..., :size], left)
        spans = out.at[..., size:].add(right[..., size:])
        levels.append(spans)
    weights = jnp.repeat(level_weight.astype(F32) * LEVEL_UNIT, BLOCK, axis=0)
    front = jnp.moveaxis(front.reshape(tokens, heads, size), 1, 0)
    added = jnp.zeros_like(front)
    for bit in range(bits):
        pick = jnp.maximum(jnp.right_shift(place, bit) - 1, 0)
        span = lax.dynamic_index_in_dim(levels[bit], pick, 0, keepdims=False)
        is_set = jnp.bitwise_and(jnp.right_shift(place, bit), 1) == 1
        out = mm(front, span)
        added = added + jnp.where(
            is_set, weights[:, 1 + depth + bit][None, :, None] * out[..., size:], 0.0
        )
        front = jnp.where(is_set, out[..., :size], front)
    heads_out = (total + jnp.moveaxis(added, 0, 1).reshape(tokens, heads * size)).astype(BF16)
    mixed_out = lax.psum_scatter(
        jnp.dot(heads_out, out_weight, preferred_element_type=F32),
        "head",
        scatter_dimension=0,
        tiled=True,
    )
    return mixed_out.astype(BF16)


def solution(mesh):
    placed = (
        P("seq", "head"),
        P("seq", "head"),
        P("seq", "head"),
        P("head", "seq"),
        P("head", "seq"),
        P("seq", None),
        P("head", None),
    )
    return jax.shard_map(
        per_device, mesh=mesh, in_specs=placed, out_specs=P(("seq", "head"), None), check_vma=False
    )
```

```python
import jax
import jax.numpy as jnp
from jax import lax
from jax.experimental import pallas as pl
from jax.experimental.pallas import tpu as pltpu
from jax.sharding import PartitionSpec as P

BLOCK = 64
NORM_EPS = 1e-06
LEVEL_UNIT = 0.125
F32 = jnp.float32
BF16 = jnp.bfloat16
MESH = pl.DeviceIdType.MESH
NN = (((1,), (0,)), ((), ()))
NT = (((1,), (1,)), ((), ()))
TN = (((0,), (0,)), ((), ()))


def dot(left, right, dims=NN):
    return lax.dot_general(left, right, dims, preferred_element_type=F32)


def exact_dot(left, right, dims=NN):
    return lax.dot_general(
        left, right, dims, precision=lax.Precision.HIGHEST, preferred_element_type=F32
    )


def split(x):
    high = x.astype(BF16)
    return high, (x - high.astype(F32)).astype(BF16)


def dot3(left, right):
    (lh, ll), (rh, rl) = left, right
    return dot(lh, rh) + (dot(lh, rl) + dot(ll, rh))


def local_kernel(q_ref, k_ref, v_ref, beta_ref, decay_ref, lw_ref, g_ref, o_ref, a_ref, b_ref):
    blocks = q_ref.shape[0] // BLOCK
    size = q_ref.shape[1]
    every = range(blocks)
    row_at = lax.broadcasted_iota(jnp.int32, (BLOCK, BLOCK), 0)
    col_at = lax.broadcasted_iota(jnp.int32, (BLOCK, BLOCK), 1)
    causal, strictly, diag = row_at >= col_at, row_at > col_at, row_at == col_at
    lower = jnp.where(causal, 1.0, 0.0).astype(F32)
    eye = jnp.where(diag, 1.0, 0.0).astype(F32)
    beta_rows = beta_ref[0]
    decay_rows = decay_ref[0]
    log_rows = -exact_dot(decay_rows, lower, NT)
    log_cols = -exact_dot(lower, decay_rows, NT)
    beta_cols = exact_dot(eye, beta_rows, NT)

    q = [q_ref[c * BLOCK : (c + 1) * BLOCK, :] for c in every]
    k = [k_ref[c * BLOCK : (c + 1) * BLOCK, :] for c in every]
    v = [v_ref[c * BLOCK : (c + 1) * BLOCK, :] for c in every]
    power, inverse, scores, pre = [], [], [], []
    for c in every:
        log_row, log_col = log_rows[c : c + 1, :], log_cols[:, c : c + 1]
        gram = dot(k[c], k[c], NT)
        on_diag = jnp.where(diag, gram, 0.0)
        rk_row = lax.rsqrt(jnp.sum(on_diag, axis=0, keepdims=True) + NORM_EPS)
        rk_col = lax.rsqrt(jnp.sum(on_diag, axis=1, keepdims=True) + NORM_EPS)
        qf = q[c].astype(F32)
        rq_col = lax.rsqrt(jnp.sum(qf * qf, axis=1, keepdims=True) + NORM_EPS)
        ratios = jnp.where(causal, jnp.exp(jnp.where(causal, log_col - log_row, 0.0)), 0.0)
        scaled = ratios * rk_row
        n = jnp.where(strictly, (beta_cols[:, c : c + 1] * rk_col) * (scaled * gram), 0.0)
        power.append(n)
        inverse.append(eye - n)
        scores.append(dot(q[c], k[c], NT) * (scaled * rq_col))
        end = log_row[:, BLOCK - 1 :]
        pre.append((
            beta_rows[c : c + 1, :] * rk_row * jnp.exp(log_row),
            beta_rows[c : c + 1, :],
            rk_col * jnp.exp(end - log_col),
            jnp.exp(log_col) * rq_col * qf,
            jnp.exp(end),
        ))
    steps = (BLOCK - 1).bit_length() - 1
    for c in every:
        ph, plo = split(power[c])
        power[c] = dot3((ph, plo), (ph, plo))
    for step in range(steps):
        for c in every:
            ph, plo = split(power[c])
            ih, ilo = split(inverse[c])
            if step < steps - 1:
                out = dot3(
                    (jnp.concatenate([ph, ih], 0), jnp.concatenate([plo, ilo], 0)), (ph, plo)
                )
                power[c] = out[:BLOCK]
                inverse[c] = inverse[c] + out[BLOCK:]
            else:
                inverse[c] = inverse[c] + dot3((ih, ilo), (ph, plo))
    maps, fronts, inside = [], [], []
    eye_state = jnp.where(
        lax.broadcasted_iota(jnp.int32, (size, size), 0)
        == lax.broadcasted_iota(jnp.int32, (size, size), 1),
        1.0,
        0.0,
    ).astype(F32)
    for c in every:
        key_scale, value_scale, tail_scale, q_part, gamma_end = pre[c]
        kh, kl = split(inverse[c] * key_scale)
        vh, vl = split(inverse[c] * value_scale)
        w = jnp.concatenate([dot(kh, k[c]) + dot(kl, k[c]), dot(vh, v[c]) + dot(vl, v[c])], 1)
        th, tl = split(w * tail_scale)
        carry = dot(k[c], th, TN) + dot(k[c], tl, TN)
        maps.append(
            jnp.concatenate([gamma_end * eye_state - carry[:, :size], carry[:, size:]], 1)
        )
        reads = dot3(split(scores[c]), split(w))
        fronts.append(q_part - reads[:, :size])
        inside.append(reads[:, size:])
    levels = [maps]
    while len(maps) > 1:
        merged = []
        for left, right in zip(maps[0::2], maps[1::2]):
            out = dot3(split(right[:, :size]), split(left))
            merged.append(
                jnp.concatenate([out[:, :size], out[:, size:] + right[:, size:]], 1)
            )
        maps = merged
        levels.append(maps)
    a_ref[0] = levels[-1][0][:, :size]
    b_ref[0] = levels[-1][0][:, size:]
    splits = [[split(m) for m in level] for level in levels[:-1]]
    for c in every:
        front = fronts[c]
        total = lw_ref[c, 0].astype(F32) * LEVEL_UNIT * inside[c]
        for bit in range(len(splits)):
            if c >> bit & 1:
                out = dot3(split(front), splits[bit][(c >> bit) - 1])
                total = total + lw_ref[c, 1 + bit].astype(F32) * LEVEL_UNIT * out[:, size:]
                front = out[:, :size]
        g_ref[c * BLOCK : (c + 1) * BLOCK, :] = front
        o_ref[c * BLOCK : (c + 1) * BLOCK, :] = total


def local_part(queries, key_rows, values, write_rate, decay_rate, level_weight):
    heads = write_rate.shape[0]
    tokens = queries.shape[0]
    size = queries.shape[1] // heads
    blocks = tokens // BLOCK
    wide = pl.BlockSpec((tokens, size), lambda h: (0, h))
    state = pl.BlockSpec((1, size, size), lambda h: (h, 0, 0))
    rates = pl.BlockSpec((1, blocks, BLOCK), lambda h: (h, 0, 0))
    return pl.pallas_call(
        local_kernel,
        grid=(heads,),
        in_specs=[wide, wide, wide, rates, rates, pl.BlockSpec(memory_space=pltpu.SMEM)],
        out_specs=[wide, wide, state, state],
        out_shape=[
            jax.ShapeDtypeStruct((tokens, heads * size), F32),
            jax.ShapeDtypeStruct((tokens, heads * size), F32),
            jax.ShapeDtypeStruct((heads, size, size), F32),
            jax.ShapeDtypeStruct((heads, size, size), F32),
        ],
        name="local_part",
    )(
        queries,
        key_rows,
        values,
        write_rate.reshape(heads, blocks, BLOCK),
        decay_rate.reshape(heads, blocks, BLOCK),
        level_weight,
    )


def merge_kernel(
    g_ref, o_ref, a_ref, b_ref, lw_ref, w_ref, out_ref,
    front, total, span_a, span_b, got_a, got_b, part, got,
    span_send, span_recv, part_send, part_recv,
):
    runs, groups = lax.axis_size("seq"), lax.axis_size("head")
    place, rank = lax.axis_index("seq"), lax.axis_index("head")
    bits = runs.bit_length() - 1
    heads, size = a_ref.shape[0], a_ref.shape[1]
    tokens = g_ref.shape[0]
    blocks = tokens // BLOCK
    depth = blocks.bit_length() - 1
    rows = tokens // groups
    pieces = got.shape[2]
    width = w_ref.shape[1] // pieces

    barrier = pltpu.get_barrier_semaphore()
    for hop in range(1, runs):
        pl.semaphore_signal(
            barrier, inc=1, device_id={"seq": lax.rem(place + hop, runs)}, device_id_type=MESH
        )
    has_below, has_above = rank > 0, rank < groups - 1

    @pl.when(has_below)
    def _():
        pl.semaphore_signal(barrier, inc=1, device_id={"head": rank - 1}, device_id_type=MESH)

    @pl.when(has_above)
    def _():
        pl.semaphore_signal(barrier, inc=1, device_id={"head": rank + 1}, device_id_type=MESH)

    pl.semaphore_wait(
        barrier, runs - 1 + has_below.astype(jnp.int32) + has_above.astype(jnp.int32)
    )

    def span_copy(level, fan, what):
        source = ((b_ref, span_b), (a_ref, span_a))[what]
        return pltpu.make_async_remote_copy(
            src_ref=source[0] if level == 0 else source[1].at[level - 1],
            dst_ref=(got_b, got_a)[what].at[level],
            send_sem=span_send.at[what, level, fan],
            recv_sem=span_recv.at[what, level],
            device_id={"seq": lax.rem(place + 1 + fan, runs)},
            device_id_type=MESH,
        )

    def own(level):
        if level == 0:
            return a_ref, b_ref
        return span_a.at[level - 1], span_b.at[level - 1]

    total[...] = o_ref[...]
    front[...] = g_ref[...]
    for level in range(bits):
        low = 2**level
        inner = place & (2 * low - 1)
        later = (place >> (level + 1)) > 0
        is_source = inner == low - 1
        bit_set = inner >= low

        @pl.when(is_source)
        def _():
            for fan in range(low):
                span_copy(level, fan, 0).start()

            @pl.when(later)
            def _():
                for fan in range(low):
                    span_copy(level, fan, 1).start()

        @pl.when(bit_set)
        def _():
            span_copy(level, 0, 0).wait_recv()

            @pl.when(later)
            def _():
                span_copy(level, 0, 1).wait_recv()

            if level < bits - 1:

                @pl.when(inner == 2 * low - 1)
                def _():
                    own_a, own_b = own(level)

                    @pl.loop(0, heads)
                    def _(h):
                        turn = split(own_a[h])
                        span_b[level, h] = dot3(turn, split(got_b[level, h])) + own_b[h]

                        @pl.when(later)
                        def _():
                            span_a[level, h] = dot3(turn, split(got_a[level, h]))

    for level in range(bits):
        low = 2**level
        inner = place & (2 * low - 1)
        later = (place >> (level + 1)) > 0

        @pl.when(inner >= low)
        def _():
            @pl.loop(0, heads)
            def _(h):
                columns = pl.ds(pl.multiple_of(h * size, size), size)
                now = split(front[:, columns])
                add = dot3(now, split(got_b[level, h]))
                for c in range(blocks):
                    at = slice(c * BLOCK, (c + 1) * BLOCK)
                    scale = lw_ref[c, 1 + depth + level].astype(F32) * LEVEL_UNIT
                    total[at, columns] = total[at, columns] + scale * add[at]

                @pl.when(later)
                def _():
                    front[:, columns] = dot3(now, split(got_a[level, h]))

        @pl.when(inner == low - 1)
        def _():
            for fan in range(low):
                span_copy(level, fan, 0).wait_send()

            @pl.when(later)
            def _():
                for fan in range(low):
                    span_copy(level, fan, 1).wait_send()

    for chunk in sorted(range(groups), key=lambda d: min(d, groups - 1 - d)):
        heads_out = total[chunk * rows : (chunk + 1) * rows, :].astype(BF16)
        for piece in range(pieces):
            part[chunk, piece] = dot(heads_out, w_ref[:, piece * width : (piece + 1) * width])

    def part_copy(way, chunk, piece):
        return pltpu.make_async_remote_copy(
            src_ref=part.at[chunk, piece],
            dst_ref=got.at[way, chunk, piece],
            send_sem=part_send.at[chunk, piece],
            recv_sem=part_recv.at[way, chunk, piece],
            device_id={"head": rank + 1 if way == 0 else rank - 1},
            device_id_type=MESH,
        )

    def pass_on(way, chunk):
        for piece in range(pieces):

            @pl.when((has_below, has_above)[way])
            def _():
                part_copy(way, chunk, piece).wait_recv()
                part[chunk, piece] = part[chunk, piece] + got[way, chunk, piece]

            part_copy(way, chunk, piece).start()

    for step in range(groups - 1):
        up, down = groups - 1 - step, step

        @pl.when(rank < up)
        def _():
            pass_on(0, up)

        @pl.when(rank > down)
        def _():
            pass_on(1, down)

    for chunk in range(groups):

        @pl.when(rank == chunk)
        def _():
            for piece in range(pieces):
                mixed = part[chunk, piece]
                if chunk > 0:
                    part_copy(0, chunk, piece).wait_recv()
                    mixed = mixed + got[0, chunk, piece]
                if chunk < groups - 1:
                    part_copy(1, chunk, piece).wait_recv()
                    mixed = mixed + got[1, chunk, piece]
                out_ref[:, piece * width : (piece + 1) * width] = mixed.astype(out_ref.dtype)

        @pl.when(rank != chunk)
        def _():
            for piece in range(pieces):
                part_copy(0, chunk, piece).wait_send()


def merge_part(front, total, pair_a, pair_b, level_weight, out_weight):
    runs, groups = lax.axis_size("seq"), lax.axis_size("head")
    bits = runs.bit_length() - 1
    tokens = front.shape[0]
    rows, width = tokens // groups, out_weight.shape[1]
    pieces = 4
    vmem = pl.BlockSpec(memory_space=pltpu.VMEM)
    dma = pltpu.SemaphoreType.DMA
    return pl.pallas_call(
        merge_kernel,
        in_specs=[vmem, vmem, vmem, vmem, pl.BlockSpec(memory_space=pltpu.SMEM), vmem],
        out_specs=vmem,
        out_shape=jax.ShapeDtypeStruct((rows, width), BF16),
        scratch_shapes=[
            pltpu.VMEM(front.shape, F32),
            pltpu.VMEM(front.shape, F32),
            pltpu.VMEM((max(bits - 1, 1),) + pair_a.shape, F32),
            pltpu.VMEM((max(bits - 1, 1),) + pair_a.shape, F32),
            pltpu.VMEM((bits,) + pair_a.shape, F32),
            pltpu.VMEM((bits,) + pair_a.shape, F32),
            pltpu.VMEM((groups, pieces, rows, width // pieces), F32),
            pltpu.VMEM((2, groups, pieces, rows, width // pieces), F32),
            dma((2, bits, runs // 2)),
            dma((2, bits)),
            dma((groups, pieces)),
            dma((2, groups, pieces)),
        ],
        compiler_params=pltpu.CompilerParams(
            collective_id=0, has_side_effects=True, vmem_limit_bytes=60 * 2**20
        ),
        name="merge_part",
    )(front, total, pair_a, pair_b, level_weight, out_weight)


def per_device(queries, key_rows, values, write_rate, decay_rate, level_weight, out_weight):
    front, total, pair_a, pair_b = local_part(
        queries, key_rows, values, write_rate, decay_rate, level_weight
    )
    return merge_part(front, total, pair_a, pair_b, level_weight, out_weight)


def solution(mesh):
    placed = (
        P("seq", "head"),
        P("seq", "head"),
        P("seq", "head"),
        P("head", "seq"),
        P("head", "seq"),
        P("seq", None),
        P("head", None),
    )
    return jax.shard_map(
        per_device, mesh=mesh, in_specs=placed, out_specs=P(("seq", "head"), None), check_vma=False
    )
```

```python
import jax
import jax.numpy as jnp
from jax import lax
from jax.experimental import pallas as pl
from jax.experimental.pallas import tpu as pltpu
from jax.sharding import PartitionSpec as P

BLOCK = 64
NORM_EPS = 1e-06
LEVEL_UNIT = 0.125
F32 = jnp.float32
BF16 = jnp.bfloat16
MESH = pl.DeviceIdType.MESH
NN = (((1,), (0,)), ((), ()))
NT = (((1,), (1,)), ((), ()))
TN = (((0,), (0,)), ((), ()))


def dot(left, right, dims=NN):
    return lax.dot_general(left, right, dims, preferred_element_type=F32)


def exact_dot(left, right, dims=NN):
    return lax.dot_general(
        left, right, dims, precision=lax.Precision.HIGHEST, preferred_element_type=F32
    )


def split(x):
    high = x.astype(BF16)
    return high, (x - high.astype(F32)).astype(BF16)


def dot3(left, right):
    (lh, ll), (rh, rl) = left, right
    return dot(lh, rh) + (dot(lh, rl) + dot(ll, rh))


def local_kernel(q_ref, k_ref, v_ref, beta_ref, decay_ref, lw_ref, g_ref, o_ref, a_ref, b_ref):
    blocks = q_ref.shape[0] // BLOCK
    size = q_ref.shape[1]
    every = range(blocks)
    row_at = lax.broadcasted_iota(jnp.int32, (BLOCK, BLOCK), 0)
    col_at = lax.broadcasted_iota(jnp.int32, (BLOCK, BLOCK), 1)
    causal, strictly, diag = row_at >= col_at, row_at > col_at, row_at == col_at
    lower = jnp.where(causal, 1.0, 0.0).astype(F32)
    eye = jnp.where(diag, 1.0, 0.0).astype(F32)
    head = pl.program_id(0)

    def block_rows(ref):
        row = ref[pl.ds(head, 1), :]
        return jnp.concatenate([row[:, c * BLOCK : (c + 1) * BLOCK] for c in every], 0)

    beta_rows, decay_rows = block_rows(beta_ref), block_rows(decay_ref)
    log_rows = -exact_dot(decay_rows, lower, NT)
    log_cols = -exact_dot(lower, decay_rows, NT)
    beta_cols = exact_dot(eye, beta_rows, NT)

    q = [q_ref[c * BLOCK : (c + 1) * BLOCK, :] for c in every]
    k = [k_ref[c * BLOCK : (c + 1) * BLOCK, :] for c in every]
    v = [v_ref[c * BLOCK : (c + 1) * BLOCK, :] for c in every]
    power, inverse, scores, pre = [], [], [], []
    for c in every:
        log_row, log_col = log_rows[c : c + 1, :], log_cols[:, c : c + 1]
        gram = dot(k[c], k[c], NT)
        on_diag = jnp.where(diag, gram, 0.0)
        rk_row = lax.rsqrt(jnp.sum(on_diag, axis=0, keepdims=True) + NORM_EPS)
        rk_col = lax.rsqrt(jnp.sum(on_diag, axis=1, keepdims=True) + NORM_EPS)
        qf = q[c].astype(F32)
        rq_col = lax.rsqrt(jnp.sum(qf * qf, axis=1, keepdims=True) + NORM_EPS)
        ratios = jnp.where(causal, jnp.exp(jnp.where(causal, log_col - log_row, 0.0)), 0.0)
        scaled = ratios * rk_row
        n = jnp.where(strictly, (beta_cols[:, c : c + 1] * rk_col) * (scaled * gram), 0.0)
        power.append(n)
        inverse.append(eye - n)
        scores.append(dot(q[c], k[c], NT) * (scaled * rq_col))
        end = log_row[:, BLOCK - 1 :]
        pre.append((
            beta_rows[c : c + 1, :] * rk_row * jnp.exp(log_row),
            beta_rows[c : c + 1, :],
            rk_col * jnp.exp(end - log_col),
            jnp.exp(log_col) * rq_col * qf,
            jnp.exp(end),
        ))
    steps = (BLOCK - 1).bit_length() - 1
    for c in every:
        ph, plo = split(power[c])
        power[c] = dot3((ph, plo), (ph, plo))
    for step in range(steps):
        for c in every:
            ph, plo = split(power[c])
            ih, ilo = split(inverse[c])
            if step < steps - 1:
                out = dot3(
                    (jnp.concatenate([ph, ih], 0), jnp.concatenate([plo, ilo], 0)), (ph, plo)
                )
                power[c] = out[:BLOCK]
                inverse[c] = inverse[c] + out[BLOCK:]
            else:
                inverse[c] = inverse[c] + dot3((ih, ilo), (ph, plo))
    maps, fronts, inside = [], [], []
    eye_state = jnp.where(
        lax.broadcasted_iota(jnp.int32, (size, size), 0)
        == lax.broadcasted_iota(jnp.int32, (size, size), 1),
        1.0,
        0.0,
    ).astype(F32)
    for c in every:
        key_scale, value_scale, tail_scale, q_part, gamma_end = pre[c]
        kh, kl = split(inverse[c] * key_scale)
        vh, vl = split(inverse[c] * value_scale)
        w = jnp.concatenate([dot(kh, k[c]) + dot(kl, k[c]), dot(vh, v[c]) + dot(vl, v[c])], 1)
        th, tl = split(w * tail_scale)
        carry = dot(k[c], th, TN) + dot(k[c], tl, TN)
        maps.append(
            jnp.concatenate([gamma_end * eye_state - carry[:, :size], carry[:, size:]], 1)
        )
        reads = dot3(split(scores[c]), split(w))
        fronts.append(q_part - reads[:, :size])
        inside.append(reads[:, size:])
    levels = [maps]
    while len(maps) > 1:
        merged = []
        for left, right in zip(maps[0::2], maps[1::2]):
            out = dot3(split(right[:, :size]), split(left))
            merged.append(
                jnp.concatenate([out[:, :size], out[:, size:] + right[:, size:]], 1)
            )
        maps = merged
        levels.append(maps)
    a_ref[0] = levels[-1][0][:, :size]
    b_ref[0] = levels[-1][0][:, size:]
    splits = [[split(m) for m in level] for level in levels[:-1]]
    for c in every:
        front = fronts[c]
        total = lw_ref[c, 0].astype(F32) * LEVEL_UNIT * inside[c]
        for bit in range(len(splits)):
            if c >> bit & 1:
                out = dot3(split(front), splits[bit][(c >> bit) - 1])
                total = total + lw_ref[c, 1 + bit].astype(F32) * LEVEL_UNIT * out[:, size:]
                front = out[:, :size]
        g_ref[c * BLOCK : (c + 1) * BLOCK, :] = front
        o_ref[c * BLOCK : (c + 1) * BLOCK, :] = total


def local_part(queries, key_rows, values, write_rate, decay_rate, level_weight):
    heads = write_rate.shape[0]
    tokens = queries.shape[0]
    size = queries.shape[1] // heads
    wide = pl.BlockSpec((tokens, size), lambda h: (0, h))
    state = pl.BlockSpec((1, size, size), lambda h: (h, 0, 0))
    rates = pl.BlockSpec((heads, tokens), lambda h: (0, 0))
    return pl.pallas_call(
        local_kernel,
        grid=(heads,),
        in_specs=[wide, wide, wide, rates, rates, pl.BlockSpec(memory_space=pltpu.SMEM)],
        out_specs=[wide, wide, state, state],
        out_shape=[
            jax.ShapeDtypeStruct((tokens, heads * size), F32),
            jax.ShapeDtypeStruct((tokens, heads * size), F32),
            jax.ShapeDtypeStruct((heads, size, size), F32),
            jax.ShapeDtypeStruct((heads, size, size), F32),
        ],
        name="local_part",
    )(
        queries,
        key_rows,
        values,
        write_rate,
        decay_rate,
        level_weight,
    )


def merge_kernel(
    g_ref, o_ref, a_ref, b_ref, lw_ref, w_ref, out_ref,
    front, total, span_a, span_b, got_a, got_b, part, got,
    span_send, span_recv, part_send, part_recv,
):
    runs, groups = lax.axis_size("seq"), lax.axis_size("head")
    place, rank = lax.axis_index("seq"), lax.axis_index("head")
    bits = runs.bit_length() - 1
    heads, size = a_ref.shape[0], a_ref.shape[1]
    tokens = g_ref.shape[0]
    blocks = tokens // BLOCK
    depth = blocks.bit_length() - 1
    rows = tokens // groups
    pieces = got.shape[2]
    width = w_ref.shape[1] // pieces

    barrier = pltpu.get_barrier_semaphore()
    for hop in range(1, runs):
        pl.semaphore_signal(
            barrier, inc=1, device_id={"seq": lax.rem(place + hop, runs)}, device_id_type=MESH
        )
    has_below, has_above = rank > 0, rank < groups - 1

    @pl.when(has_below)
    def _():
        pl.semaphore_signal(barrier, inc=1, device_id={"head": rank - 1}, device_id_type=MESH)

    @pl.when(has_above)
    def _():
        pl.semaphore_signal(barrier, inc=1, device_id={"head": rank + 1}, device_id_type=MESH)

    pl.semaphore_wait(
        barrier, runs - 1 + has_below.astype(jnp.int32) + has_above.astype(jnp.int32)
    )

    def receivers(level):
        return range(1) if level == 0 else range(1, 2**level, 2)

    def relay_copy(level, what):
        held = (got_b, got_a)[what].at[level]
        return pltpu.make_async_remote_copy(
            src_ref=held,
            dst_ref=held,
            send_sem=span_send.at[what, level, 0],
            recv_sem=span_recv.at[what, level],
            device_id={"seq": lax.rem(place + runs - 1, runs)},
            device_id_type=MESH,
        )

    def span_copy(level, fan, what):
        source = ((b_ref, span_b), (a_ref, span_a))[what]
        return pltpu.make_async_remote_copy(
            src_ref=source[0] if level == 0 else source[1].at[level - 1],
            dst_ref=(got_b, got_a)[what].at[level],
            send_sem=span_send.at[what, level, fan],
            recv_sem=span_recv.at[what, level],
            device_id={"seq": lax.rem(place + 1 + fan, runs)},
            device_id_type=MESH,
        )

    def own(level):
        if level == 0:
            return a_ref, b_ref
        return span_a.at[level - 1], span_b.at[level - 1]

    total[...] = o_ref[...]
    front[...] = g_ref[...]
    for level in range(bits):
        low = 2**level
        inner = place & (2 * low - 1)
        later = (place >> (level + 1)) > 0
        is_source = inner == low - 1
        bit_set = inner >= low

        @pl.when(is_source)
        def _():
            for fan in receivers(level):
                span_copy(level, fan, 0).start()

            @pl.when(later)
            def _():
                for fan in receivers(level):
                    span_copy(level, fan, 1).start()

        @pl.when(bit_set)
        def _():
            span_copy(level, 0, 0).wait_recv()
            if level > 0:

                @pl.when(place & 1 == 1)
                def _():
                    relay_copy(level, 0).start()

            @pl.when(later)
            def _():
                span_copy(level, 0, 1).wait_recv()
                if level > 0:

                    @pl.when(place & 1 == 1)
                    def _():
                        relay_copy(level, 1).start()

            if level < bits - 1:

                @pl.when(inner == 2 * low - 1)
                def _():
                    own_a, own_b = own(level)

                    @pl.loop(0, heads)
                    def _(h):
                        turn = split(own_a[h])
                        span_b[level, h] = dot3(turn, split(got_b[level, h])) + own_b[h]

                        @pl.when(later)
                        def _():
                            span_a[level, h] = dot3(turn, split(got_a[level, h]))

    for level in range(bits):
        low = 2**level
        inner = place & (2 * low - 1)
        later = (place >> (level + 1)) > 0

        @pl.when(inner >= low)
        def _():
            @pl.loop(0, heads)
            def _(h):
                columns = pl.ds(pl.multiple_of(h * size, size), size)
                now = split(front[:, columns])
                add = dot3(now, split(got_b[level, h]))
                for c in range(blocks):
                    at = slice(c * BLOCK, (c + 1) * BLOCK)
                    scale = lw_ref[c, 1 + depth + level].astype(F32) * LEVEL_UNIT
                    total[at, columns] = total[at, columns] + scale * add[at]

                @pl.when(later)
                def _():
                    front[:, columns] = dot3(now, split(got_a[level, h]))

        if level > 0:

            @pl.when((inner >= low) & (place & 1 == 1))
            def _():
                relay_copy(level, 0).wait_send()

                @pl.when(later)
                def _():
                    relay_copy(level, 1).wait_send()

        @pl.when(inner == low - 1)
        def _():
            for fan in receivers(level):
                span_copy(level, fan, 0).wait_send()

            @pl.when(later)
            def _():
                for fan in receivers(level):
                    span_copy(level, fan, 1).wait_send()

    def own_part(chunk, piece):
        heads_out = total[chunk * rows : (chunk + 1) * rows, :].astype(BF16)
        return dot(heads_out, w_ref[:, piece * width : (piece + 1) * width])

    def part_copy(way, chunk, piece):
        return pltpu.make_async_remote_copy(
            src_ref=part.at[chunk, piece],
            dst_ref=got.at[way, chunk, piece],
            send_sem=part_send.at[chunk, piece],
            recv_sem=part_recv.at[way, chunk, piece],
            device_id={"head": rank + 1 if way == 0 else rank - 1},
            device_id_type=MESH,
        )

    def pass_on(way, chunk):
        for piece in range(pieces):
            part[chunk, piece] = own_part(chunk, piece)

            @pl.when((has_below, has_above)[way])
            def _():
                part_copy(way, chunk, piece).wait_recv()
                part[chunk, piece] = part[chunk, piece] + got[way, chunk, piece]

            part_copy(way, chunk, piece).start()

    for step in range(groups - 1):
        up, down = groups - 1 - step, step

        @pl.when(rank < up)
        def _():
            pass_on(0, up)

        @pl.when(rank > down)
        def _():
            pass_on(1, down)

    for chunk in range(groups):

        @pl.when(rank == chunk)
        def _():
            for piece in range(pieces):
                mixed = own_part(chunk, piece)
                if chunk > 0:
                    part_copy(0, chunk, piece).wait_recv()
                    mixed = mixed + got[0, chunk, piece]
                if chunk < groups - 1:
                    part_copy(1, chunk, piece).wait_recv()
                    mixed = mixed + got[1, chunk, piece]
                out_ref[:, piece * width : (piece + 1) * width] = mixed.astype(out_ref.dtype)

        @pl.when(rank != chunk)
        def _():
            for piece in range(pieces):
                part_copy(0, chunk, piece).wait_send()


def merge_part(front, total, pair_a, pair_b, level_weight, out_weight):
    runs, groups = lax.axis_size("seq"), lax.axis_size("head")
    bits = runs.bit_length() - 1
    tokens = front.shape[0]
    rows, width = tokens // groups, out_weight.shape[1]
    pieces = 4
    vmem = pl.BlockSpec(memory_space=pltpu.VMEM)
    dma = pltpu.SemaphoreType.DMA
    return pl.pallas_call(
        merge_kernel,
        in_specs=[vmem, vmem, vmem, vmem, pl.BlockSpec(memory_space=pltpu.SMEM), vmem],
        out_specs=vmem,
        out_shape=jax.ShapeDtypeStruct((rows, width), BF16),
        scratch_shapes=[
            pltpu.VMEM(front.shape, F32),
            pltpu.VMEM(front.shape, F32),
            pltpu.VMEM((max(bits - 1, 1),) + pair_a.shape, F32),
            pltpu.VMEM((max(bits - 1, 1),) + pair_a.shape, F32),
            pltpu.VMEM((bits,) + pair_a.shape, F32),
            pltpu.VMEM((bits,) + pair_a.shape, F32),
            pltpu.VMEM((groups, pieces, rows, width // pieces), F32),
            pltpu.VMEM((2, groups, pieces, rows, width // pieces), F32),
            dma((2, bits, runs // 2)),
            dma((2, bits)),
            dma((groups, pieces)),
            dma((2, groups, pieces)),
        ],
        compiler_params=pltpu.CompilerParams(
            collective_id=0, has_side_effects=True, vmem_limit_bytes=60 * 2**20
        ),
        name="merge_part",
    )(front, total, pair_a, pair_b, level_weight, out_weight)


def per_device(queries, key_rows, values, write_rate, decay_rate, level_weight, out_weight):
    front, total, pair_a, pair_b = local_part(
        queries, key_rows, values, write_rate, decay_rate, level_weight
    )
    return merge_part(front, total, pair_a, pair_b, level_weight, out_weight)


def solution(mesh):
    placed = (
        P("seq", "head"),
        P("seq", "head"),
        P("seq", "head"),
        P("head", "seq"),
        P("head", "seq"),
        P("seq", None),
        P("head", None),
    )
    return jax.shard_map(
        per_device, mesh=mesh, in_specs=placed, out_specs=P(("seq", "head"), None), check_vma=False
    )
```

```python
import jax
import jax.numpy as jnp
from jax import lax
from jax.experimental import pallas as pl
from jax.experimental.pallas import tpu as pltpu
from jax.sharding import PartitionSpec as P

BLOCK = 64
NORM_EPS = 1e-06
LEVEL_UNIT = 0.125
F32 = jnp.float32
BF16 = jnp.bfloat16
MESH = pl.DeviceIdType.MESH
NN = (((1,), (0,)), ((), ()))
NT = (((1,), (1,)), ((), ()))
TN = (((0,), (0,)), ((), ()))


def dot(left, right, dims=NN):
    return lax.dot_general(left, right, dims, preferred_element_type=F32)


def exact_dot(left, right, dims=NN):
    return lax.dot_general(
        left, right, dims, precision=lax.Precision.HIGHEST, preferred_element_type=F32
    )


def split(x):
    high = x.astype(BF16)
    return high, (x - high.astype(F32)).astype(BF16)


def dot3(left, right):
    (lh, ll), (rh, rl) = left, right
    return dot(lh, rh) + (dot(lh, rl) + dot(ll, rh))


def local_kernel(q_ref, k_ref, v_ref, beta_ref, decay_ref, lw_ref, g_ref, o_ref, a_ref, b_ref):
    blocks = q_ref.shape[0] // BLOCK
    size = q_ref.shape[1]
    every = range(blocks)
    row_at = lax.broadcasted_iota(jnp.int32, (BLOCK, BLOCK), 0)
    col_at = lax.broadcasted_iota(jnp.int32, (BLOCK, BLOCK), 1)
    causal, strictly, diag = row_at >= col_at, row_at > col_at, row_at == col_at
    lower = jnp.where(causal, 1.0, 0.0).astype(F32)
    eye = jnp.where(diag, 1.0, 0.0).astype(F32)
    head = pl.program_id(0)

    def block_rows(ref):
        row = ref[pl.ds(head, 1), :]
        return jnp.concatenate([row[:, c * BLOCK : (c + 1) * BLOCK] for c in every], 0)

    beta_rows, decay_rows = block_rows(beta_ref), block_rows(decay_ref)
    log_rows = -exact_dot(decay_rows, lower, NT)
    log_cols = -exact_dot(lower, decay_rows, NT)
    beta_cols = exact_dot(eye, beta_rows, NT)

    q = [q_ref[c * BLOCK : (c + 1) * BLOCK, :] for c in every]
    k = [k_ref[c * BLOCK : (c + 1) * BLOCK, :] for c in every]
    v = [v_ref[c * BLOCK : (c + 1) * BLOCK, :] for c in every]
    power, inverse, scores, pre = [], [], [], []
    for c in every:
        log_row, log_col = log_rows[c : c + 1, :], log_cols[:, c : c + 1]
        gram = dot(k[c], k[c], NT)
        on_diag = jnp.where(diag, gram, 0.0)
        rk_row = lax.rsqrt(jnp.sum(on_diag, axis=0, keepdims=True) + NORM_EPS)
        rk_col = lax.rsqrt(jnp.sum(on_diag, axis=1, keepdims=True) + NORM_EPS)
        qf = q[c].astype(F32)
        rq_col = lax.rsqrt(jnp.sum(qf * qf, axis=1, keepdims=True) + NORM_EPS)
        ratios = jnp.where(causal, jnp.exp(jnp.where(causal, log_col - log_row, 0.0)), 0.0)
        scaled = ratios * rk_row
        n = jnp.where(strictly, (beta_cols[:, c : c + 1] * rk_col) * (scaled * gram), 0.0)
        power.append(n)
        inverse.append(eye - n)
        scores.append(dot(q[c], k[c], NT) * (scaled * rq_col))
        end = log_row[:, BLOCK - 1 :]
        pre.append((
            beta_rows[c : c + 1, :] * rk_row * jnp.exp(log_row),
            beta_rows[c : c + 1, :],
            rk_col * jnp.exp(end - log_col),
            jnp.exp(log_col) * rq_col * qf,
            jnp.exp(end),
        ))
    steps = (BLOCK - 1).bit_length() - 1
    for c in every:
        ph, plo = split(power[c])
        power[c] = dot3((ph, plo), (ph, plo))
    for step in range(steps):
        for c in every:
            ph, plo = split(power[c])
            ih, ilo = split(inverse[c])
            if step < steps - 1:
                out = dot3(
                    (jnp.concatenate([ph, ih], 0), jnp.concatenate([plo, ilo], 0)), (ph, plo)
                )
                power[c] = out[:BLOCK]
                inverse[c] = inverse[c] + out[BLOCK:]
            else:
                inverse[c] = inverse[c] + dot3((ih, ilo), (ph, plo))
    maps, fronts, inside = [], [], []
    eye_state = jnp.where(
        lax.broadcasted_iota(jnp.int32, (size, size), 0)
        == lax.broadcasted_iota(jnp.int32, (size, size), 1),
        1.0,
        0.0,
    ).astype(F32)
    for c in every:
        key_scale, value_scale, tail_scale, q_part, gamma_end = pre[c]
        kh, kl = split(inverse[c] * key_scale)
        vh, vl = split(inverse[c] * value_scale)
        w = jnp.concatenate([dot(kh, k[c]) + dot(kl, k[c]), dot(vh, v[c]) + dot(vl, v[c])], 1)
        th, tl = split(w * tail_scale)
        carry = dot(k[c], th, TN) + dot(k[c], tl, TN)
        maps.append(
            jnp.concatenate([gamma_end * eye_state - carry[:, :size], carry[:, size:]], 1)
        )
        reads = dot3(split(scores[c]), split(w))
        fronts.append(q_part - reads[:, :size])
        inside.append(reads[:, size:])
    levels = [maps]
    while len(maps) > 1:
        merged = []
        for left, right in zip(maps[0::2], maps[1::2]):
            out = dot3(split(right[:, :size]), split(left))
            merged.append(
                jnp.concatenate([out[:, :size], out[:, size:] + right[:, size:]], 1)
            )
        maps = merged
        levels.append(maps)
    a_ref[0] = levels[-1][0][:, :size]
    b_ref[0] = levels[-1][0][:, size:]
    splits = [[split(m) for m in level] for level in levels[:-1]]
    for c in every:
        front = fronts[c]
        total = lw_ref[c, 0].astype(F32) * LEVEL_UNIT * inside[c]
        for bit in range(len(splits)):
            if c >> bit & 1:
                out = dot3(split(front), splits[bit][(c >> bit) - 1])
                total = total + lw_ref[c, 1 + bit].astype(F32) * LEVEL_UNIT * out[:, size:]
                front = out[:, :size]
        g_ref[c * BLOCK : (c + 1) * BLOCK, :] = front
        o_ref[c * BLOCK : (c + 1) * BLOCK, :] = total


def local_part(queries, key_rows, values, write_rate, decay_rate, level_weight):
    heads = write_rate.shape[0]
    tokens = queries.shape[0]
    size = queries.shape[1] // heads
    wide = pl.BlockSpec((tokens, size), lambda h: (0, h))
    state = pl.BlockSpec((1, size, size), lambda h: (h, 0, 0))
    rates = pl.BlockSpec((heads, tokens), lambda h: (0, 0))
    return pl.pallas_call(
        local_kernel,
        grid=(heads,),
        in_specs=[wide, wide, wide, rates, rates, pl.BlockSpec(memory_space=pltpu.SMEM)],
        out_specs=[wide, wide, state, state],
        out_shape=[
            jax.ShapeDtypeStruct((tokens, heads * size), F32),
            jax.ShapeDtypeStruct((tokens, heads * size), F32),
            jax.ShapeDtypeStruct((heads, size, size), F32),
            jax.ShapeDtypeStruct((heads, size, size), F32),
        ],
        name="local_part",
    )(
        queries,
        key_rows,
        values,
        write_rate,
        decay_rate,
        level_weight,
    )


def merge_kernel(
    g_ref, o_ref, a_ref, b_ref, lw_ref, w_ref, out_ref,
    front, total, span_a, span_b, got_a, got_b, part, got,
    span_send, span_recv, part_send, part_recv,
):
    runs, groups = lax.axis_size("seq"), lax.axis_size("head")
    place, rank = lax.axis_index("seq"), lax.axis_index("head")
    bits = runs.bit_length() - 1
    heads, size = a_ref.shape[0], a_ref.shape[1]
    tokens = g_ref.shape[0]
    blocks = tokens // BLOCK
    depth = blocks.bit_length() - 1
    rows = tokens // groups
    pieces = got.shape[2]
    width = w_ref.shape[1] // pieces

    barrier = pltpu.get_barrier_semaphore()
    for hop in range(1, runs):
        pl.semaphore_signal(
            barrier, inc=1, device_id={"seq": lax.rem(place + hop, runs)}, device_id_type=MESH
        )
    has_below, has_above = rank > 0, rank < groups - 1

    @pl.when(has_below)
    def _():
        pl.semaphore_signal(barrier, inc=1, device_id={"head": rank - 1}, device_id_type=MESH)

    @pl.when(has_above)
    def _():
        pl.semaphore_signal(barrier, inc=1, device_id={"head": rank + 1}, device_id_type=MESH)

    pl.semaphore_wait(
        barrier, runs - 1 + has_below.astype(jnp.int32) + has_above.astype(jnp.int32)
    )

    def receivers(level):
        return range(1) if level == 0 else range(1, 2**level, 2)

    def relay_copy(level, what):
        held = (got_b, got_a)[what].at[level]
        return pltpu.make_async_remote_copy(
            src_ref=held,
            dst_ref=held,
            send_sem=span_send.at[what, level, 0],
            recv_sem=span_recv.at[what, level],
            device_id={"seq": lax.rem(place + runs - 1, runs)},
            device_id_type=MESH,
        )

    def span_copy(level, fan, what):
        source = ((b_ref, span_b), (a_ref, span_a))[what]
        return pltpu.make_async_remote_copy(
            src_ref=source[0] if level == 0 else source[1].at[level - 1],
            dst_ref=(got_b, got_a)[what].at[level],
            send_sem=span_send.at[what, level, fan],
            recv_sem=span_recv.at[what, level],
            device_id={"seq": lax.rem(place + 1 + fan, runs)},
            device_id_type=MESH,
        )

    def own(level):
        if level == 0:
            return a_ref, b_ref
        return span_a.at[level - 1], span_b.at[level - 1]

    total[...] = o_ref[...]
    front[...] = g_ref[...]
    for level in range(bits):
        low = 2**level
        inner = place & (2 * low - 1)
        later = (place >> (level + 1)) > 0
        is_source = inner == low - 1
        bit_set = inner >= low

        @pl.when(is_source)
        def _():
            for fan in receivers(level):
                span_copy(level, fan, 0).start()

            @pl.when(later)
            def _():
                for fan in receivers(level):
                    span_copy(level, fan, 1).start()

        @pl.when(bit_set)
        def _():
            span_copy(level, 0, 0).wait_recv()
            if level > 0:

                @pl.when(place & 1 == 1)
                def _():
                    relay_copy(level, 0).start()

            @pl.when(later)
            def _():
                span_copy(level, 0, 1).wait_recv()
                if level > 0:

                    @pl.when(place & 1 == 1)
                    def _():
                        relay_copy(level, 1).start()

            if level < bits - 1:

                @pl.when(inner == 2 * low - 1)
                def _():
                    own_a, own_b = own(level)

                    @pl.loop(0, heads)
                    def _(h):
                        turn = split(own_a[h])
                        span_b[level, h] = dot3(turn, split(got_b[level, h])) + own_b[h]

                        @pl.when(later)
                        def _():
                            span_a[level, h] = dot3(turn, split(got_a[level, h]))

    for level in range(bits):
        low = 2**level
        inner = place & (2 * low - 1)
        later = (place >> (level + 1)) > 0

        @pl.when(inner >= low)
        def _():
            @pl.loop(0, heads)
            def _(h):
                columns = pl.ds(pl.multiple_of(h * size, size), size)
                now = split(front[:, columns])
                add = dot3(now, split(got_b[level, h]))
                for c in range(blocks):
                    at = slice(c * BLOCK, (c + 1) * BLOCK)
                    scale = lw_ref[c, 1 + depth + level].astype(F32) * LEVEL_UNIT
                    total[at, columns] = total[at, columns] + scale * add[at]

                @pl.when(later)
                def _():
                    front[:, columns] = dot3(now, split(got_a[level, h]))

        if level > 0:

            @pl.when((inner >= low) & (place & 1 == 1))
            def _():
                relay_copy(level, 0).wait_send()

                @pl.when(later)
                def _():
                    relay_copy(level, 1).wait_send()

        @pl.when(inner == low - 1)
        def _():
            for fan in receivers(level):
                span_copy(level, fan, 0).wait_send()

            @pl.when(later)
            def _():
                for fan in receivers(level):
                    span_copy(level, fan, 1).wait_send()

    def own_part(chunk, piece):
        heads_out = total[chunk * rows : (chunk + 1) * rows, :].astype(BF16)
        return dot(heads_out, w_ref[:, piece * width : (piece + 1) * width])

    def part_copy(way, chunk, piece):
        return pltpu.make_async_remote_copy(
            src_ref=part.at[chunk, piece],
            dst_ref=got.at[way, chunk, piece],
            send_sem=part_send.at[chunk, piece],
            recv_sem=part_recv.at[way, chunk, piece],
            device_id={"head": rank + 1 if way == 0 else rank - 1},
            device_id_type=MESH,
        )

    def pass_on(here, way, chunk, piece):
        mine = own_part(chunk, piece)
        if (here > 0, here < groups - 1)[way]:
            part_copy(way, chunk, piece).wait_recv()
            mine = mine + got[way, chunk, piece]
        part[chunk, piece] = mine
        part_copy(way, chunk, piece).start()

    for here in range(groups):
        ups = [(d, p) for d in range(groups - 1, here, -1) for p in range(pieces)]
        downs = [(d, p) for d in range(here) for p in range(pieces)]
        order = [(i + 1.5 * here, 0, d, p) for i, (d, p) in enumerate(ups)]
        order += [(i + 1.5 * (groups - 1 - here), 1, d, p) for i, (d, p) in enumerate(downs)]

        @pl.when(rank == here)
        def _():
            for _, way, chunk, piece in sorted(order):
                pass_on(here, way, chunk, piece)
            for piece in range(pieces):
                mixed = own_part(here, piece)
                if here > 0:
                    part_copy(0, here, piece).wait_recv()
                    mixed = mixed + got[0, here, piece]
                if here < groups - 1:
                    part_copy(1, here, piece).wait_recv()
                    mixed = mixed + got[1, here, piece]
                out_ref[:, piece * width : (piece + 1) * width] = mixed.astype(out_ref.dtype)
            for _, way, chunk, piece in order:
                part_copy(way, chunk, piece).wait_send()


def merge_part(front, total, pair_a, pair_b, level_weight, out_weight):
    runs, groups = lax.axis_size("seq"), lax.axis_size("head")
    bits = runs.bit_length() - 1
    tokens = front.shape[0]
    rows, width = tokens // groups, out_weight.shape[1]
    pieces = 4
    vmem = pl.BlockSpec(memory_space=pltpu.VMEM)
    dma = pltpu.SemaphoreType.DMA
    return pl.pallas_call(
        merge_kernel,
        in_specs=[vmem, vmem, vmem, vmem, pl.BlockSpec(memory_space=pltpu.SMEM), vmem],
        out_specs=vmem,
        out_shape=jax.ShapeDtypeStruct((rows, width), BF16),
        scratch_shapes=[
            pltpu.VMEM(front.shape, F32),
            pltpu.VMEM(front.shape, F32),
            pltpu.VMEM((max(bits - 1, 1),) + pair_a.shape, F32),
            pltpu.VMEM((max(bits - 1, 1),) + pair_a.shape, F32),
            pltpu.VMEM((bits,) + pair_a.shape, F32),
            pltpu.VMEM((bits,) + pair_a.shape, F32),
            pltpu.VMEM((groups, pieces, rows, width // pieces), F32),
            pltpu.VMEM((2, groups, pieces, rows, width // pieces), F32),
            dma((2, bits, runs // 2)),
            dma((2, bits)),
            dma((groups, pieces)),
            dma((2, groups, pieces)),
        ],
        compiler_params=pltpu.CompilerParams(
            collective_id=0, has_side_effects=True, vmem_limit_bytes=60 * 2**20
        ),
        name="merge_part",
    )(front, total, pair_a, pair_b, level_weight, out_weight)


def per_device(queries, key_rows, values, write_rate, decay_rate, level_weight, out_weight):
    front, total, pair_a, pair_b = local_part(
        queries, key_rows, values, write_rate, decay_rate, level_weight
    )
    return merge_part(front, total, pair_a, pair_b, level_weight, out_weight)


def solution(mesh):
    placed = (
        P("seq", "head"),
        P("seq", "head"),
        P("seq", "head"),
        P("head", "seq"),
        P("head", "seq"),
        P("seq", None),
        P("head", None),
    )
    return jax.shard_map(
        per_device, mesh=mesh, in_specs=placed, out_specs=P(("seq", "head"), None), check_vma=False
    )
```
